32 devices in a mesh: parts: 2 (over y), wide: 4 (over z), narrow: 4 (over x, core).
Axes of the slice: x: 2, y: 2, z: 4, core: 2. Of those that a mesh axis runs over, the one named last changes fastest.
Arguments:
- teacher: bfloat16 [4096, 4096], P(('parts', 'wide', 'narrow')), parts along dimension 0, may hold values from -6 to 6
- weight: float32 [4096, 256], replicated, may hold values from -0.09375 to 0.09375
- block_mask: int32 [8, 4], P('parts'), parts along dimension 0, may hold values 0 or 1
- item_group: int32 [4096], P(('parts', 'wide', 'narrow')), parts along dimension 0, may hold values from 0 to 7
Outputs:
- grad_weight: float32 [8192, 256], P(('parts', 'wide', 'narrow')), parts along dimension 0
The draws below stay inside these ranges and needn't reach their ends.
There are 2 independent parts, one for each index of `parts`. The reference program is written for one: setup_inputs(seed, part) draws one part's arguments, and reference() takes and returns one part's arrays. A program takes and returns all parts, laid end to end along the dimension named above; an argument that names none is the same for every part. Nothing has to cross between parts.
Inputs may be any that keep to these rules, and one draw needn't show every extreme that they name: `block_mask`: 0 or 1 for each ordered pair of blocks.
All inputs are finite; a program needn't handle non-finite values.
Results may differ from the reference program's by a relative error of at most 0.0083.
Values may be sent and summed in bfloat16 or wider, within the bound.
A program may use at most 64 MiB of HBM per device.

```python
import jax
import jax.numpy as jnp
from jax import lax

D = 4096
P_SIZE = 256
GROUPS = 8
BLOCK = 512
BLOCKS = 4
N_ITEMS = 2048


def touch_ends(result, own_key, low, largest):
    shape = result.shape
    index_at = [jax.random.randint(jax.random.fold_in(own_key, axis), (), 0, shape[axis]) for axis in range(len(shape))]
    result = result.at[tuple(index_at)].set(low)
    longest = shape.index(max(shape))
    index_at[longest] = (index_at[longest] + 1) % shape[longest]
    return result.at[tuple(index_at)].set(largest)


def block_scale(stream_key, shape, pieces, smallest, top_value):
    def one(axis_at, parts):
        heights = jax.random.uniform(jax.random.fold_in(jax.random.fold_in(stream_key, 6), axis_at), (parts,), jnp.float32, smallest / len(pieces), top_value / len(pieces))
        return jnp.repeat(jnp.exp(heights), shape[axis_at] // parts).reshape((-1,) + (1,) * (len(shape) - axis_at - 1))

    factor_of = one(*pieces[0])
    for cut in pieces[1:]:
        factor_of = factor_of * one(*cut)
    return factor_of


def normal_values(stream_key, dims, width, most, cuts=(), dtype=jnp.bfloat16):
    values = jax.random.normal(stream_key, dims, jnp.float32) * width
    if len(cuts) > 0:
        values = block_scale(stream_key, dims, cuts, -0.22, 0.18) * values
    return jnp.clip(values, min=-most, max=most).astype(dtype)


def setup_inputs(seed: int = 0, part: int = 0) -> dict:
    key_list = jax.random.split(jax.random.key(seed), 5)
    part_keys = jax.random.split(jax.random.fold_in(key_list[4], part), 5)
    return {
        "teacher": normal_values(part_keys[0], (N_ITEMS, D), 1.0, 6.0, ((0, 16),)),
        "weight": normal_values(key_list[1], (D, P_SIZE), D ** -0.5, 0.09375, (), jnp.float32),
        "block_mask": touch_ends((jax.random.randint(part_keys[2], (BLOCKS, BLOCKS), 0, 2) < 1).astype(jnp.int32), jax.random.fold_in(part_keys[2], 1), 0, 1),
        "item_group": touch_ends(jax.random.randint(part_keys[3], (N_ITEMS,), 0, GROUPS), jax.random.fold_in(part_keys[3], 1), 0, GROUPS - 1).astype(jnp.int32),
    }


def reference(teacher, weight, block_mask, item_group):
    total = teacher.shape[0]
    low_weight = weight.astype(jnp.bfloat16)
    student = jnp.dot(teacher, low_weight, preferred_element_type=jnp.float32).astype(jnp.bfloat16)
    block_of = (jnp.arange(total) // BLOCK).astype(jnp.int32)
    mask_sym = (block_mask + block_mask.T).astype(jnp.float32)
    coef = 2.0 * D / (total * P_SIZE)

    def block_rows(index):
        start = (index * BLOCK).astype(jnp.int32)
        rows_t = lax.dynamic_slice_in_dim(teacher, start, BLOCK, 0)
        rows_s = lax.dynamic_slice_in_dim(student, start, BLOCK, 0)
        rows_g = lax.dynamic_slice_in_dim(item_group, start, BLOCK, 0)
        teach = lax.dot_general(rows_t, teacher, (((1,), (1,)), ((), ())), preferred_element_type=jnp.float32) / D
        stud = lax.dot_general(rows_s, student, (((1,), (1,)), ((), ())), preferred_element_type=jnp.float32) / P_SIZE
        pair_weight = mask_sym[index][block_of]
        same = (rows_g[:, None] == item_group[None, :]).astype(jnp.float32)
        pair_term = (pair_weight[None, :] * (1.0 + same) * (stud - teach)).astype(jnp.bfloat16)
        return (coef * jnp.dot(pair_term, student, preferred_element_type=jnp.float32)).astype(jnp.bfloat16)

    grad_student = lax.map(block_rows, jnp.arange(total // BLOCK).astype(jnp.int32)).reshape(total, P_SIZE)
    return lax.dot_general(teacher, grad_student, (((0,), (0,)), ((), ())), preferred_element_type=jnp.float32)
```

```python
import functools

import jax
import jax.numpy as jnp
from jax import lax
from jax.experimental import pallas as pl
from jax.experimental.pallas import tpu as pltpu
from jax.sharding import PartitionSpec as P

AXES = ("wide", "narrow")
NT = (((1,), (1,)), ((), ()))
TN = (((0,), (0,)), ((), ()))


def pair_kernel(block, blocks, mask_ref, rows_ref, all_ref, stud_ref, gcol_ref, grow_ref, out_ref):
    tile = rows_ref.shape[0]
    mine = pl.program_id(0) * tile // block
    rows = rows_ref[...]
    gcol = gcol_ref[...]

    def step(b, acc):
        cols = pl.ds(pl.multiple_of(b * block, block), block)
        e = lax.dot_general(rows, all_ref[cols, :], NT, preferred_element_type=jnp.float32)
        f = mask_ref[mine, b]
        w = jnp.where(gcol == grow_ref[:, cols], 2.0 * f, f)
        p = (e * w).astype(jnp.bfloat16)
        return acc + jnp.dot(p, stud_ref[cols, :], preferred_element_type=jnp.float32)

    acc = lax.fori_loop(
        0, blocks, step, jnp.zeros((tile, stud_ref.shape[1]), jnp.float32), unroll=blocks <= 4
    )
    out_ref[...] = acc.astype(jnp.bfloat16)


def pair_part(mask_sym, columns, student, group, block):
    n, dc = columns.shape
    p = student.shape[1]
    tile = block // 2
    blocks = n // block
    whole = lambda i: (0, 0)
    mine = lambda i: (i, 0)
    return pl.pallas_call(
        functools.partial(pair_kernel, block, blocks),
        grid=(n // tile,),
        in_specs=[
            pl.BlockSpec(memory_space=pltpu.SMEM),
            pl.BlockSpec((tile, dc), mine),
            pl.BlockSpec((n, dc), whole),
            pl.BlockSpec((n, p), whole),
            pl.BlockSpec((tile, 1), mine),
            pl.BlockSpec((1, n), whole),
        ],
        out_specs=pl.BlockSpec((tile, p), mine),
        out_shape=jax.ShapeDtypeStruct((n, p), jnp.bfloat16),
        compiler_params=pltpu.CompilerParams(vmem_limit_bytes=48 * 2**20),
        cost_estimate=pl.CostEstimate(
            flops=2 * n * n * (dc + p), bytes_accessed=2 * n * (dc + 2 * p), transcendentals=0
        ),
    )(mask_sym, columns, columns, student, group.reshape(n, 1), group.reshape(1, n))


def per_device(teacher, weight, block_mask, item_group):
    rows, d = teacher.shape
    width = weight.shape[1]
    wide = lax.axis_size("wide")
    count = wide * lax.axis_size("narrow")
    block = rows * lax.axis_size("narrow")
    n = rows * count
    here = lax.axis_index("wide")
    columns = lax.all_to_all(teacher, AXES, split_axis=1, concat_axis=0, tiled=True)
    group = lax.all_gather(item_group, AXES, axis=0, tiled=True)
    own = jnp.dot(
        teacher, weight.astype(jnp.bfloat16), preferred_element_type=jnp.float32
    ).astype(jnp.bfloat16)
    student = lax.all_gather(own, AXES, axis=0, tiled=True)
    mask = block_mask.astype(jnp.float32)
    mask_sym = mask + mask.T
    mine = lax.dynamic_index_in_dim(mask_sym, here, 0, keepdims=False)
    per_item = jnp.broadcast_to((mine / width)[:, None], (wide, block)).reshape(1, n)
    same = (item_group[:, None] == group[None, :]).astype(jnp.float32)
    stud = lax.dot_general(own, student, NT, preferred_element_type=jnp.float32)
    near = jnp.dot(
        (per_item * (1.0 + same) * stud).astype(jnp.bfloat16),
        student,
        preferred_element_type=jnp.float32,
    )
    far = pair_part(mask_sym * (-1.0 / d), columns, student, group, block)
    far = lax.all_to_all(far.reshape(count, rows, width), AXES, split_axis=0, concat_axis=0, tiled=True)
    total = near + jnp.sum(far.astype(jnp.float32), axis=0)
    grad = (total * (2.0 * d / (n * width))).astype(jnp.bfloat16)
    grad = lax.all_gather(grad, AXES, axis=0, tiled=True)
    return lax.dot_general(columns, grad, TN, preferred_element_type=jnp.float32)


def solution(mesh):
    in_specs = (P(("parts",) + AXES, None), P(), P("parts", None), P(("parts",) + AXES))
    return jax.shard_map(
        per_device,
        mesh=mesh,
        in_specs=in_specs,
        out_specs=P(("parts",) + AXES, None),
        check_vma=False,
    )
```

```python
import functools

import jax
import jax.numpy as jnp
from jax import lax
from jax.experimental import pallas as pl
from jax.experimental.pallas import tpu as pltpu
from jax.sharding import PartitionSpec as P

AXES = ("wide", "narrow")
NT = (((1,), (1,)), ((), ()))
TN = (((0,), (0,)), ((), ()))


def pair_kernel(block, blocks, mask_ref, rows_ref, all_ref, stud_ref, gcol_ref, grow_ref, out_ref):
    tile = rows_ref.shape[0]
    mine = pl.program_id(0) * tile // block
    rows = rows_ref[...]
    gcol = gcol_ref[...]

    def step(b, acc):
        cols = pl.ds(pl.multiple_of(b * block, block), block)
        e = lax.dot_general(rows, all_ref[cols, :], NT, preferred_element_type=jnp.float32)
        f = mask_ref[mine, b]
        w = jnp.where(gcol == grow_ref[:, cols], 2.0 * f, f)
        p = (e * w).astype(jnp.bfloat16)
        return acc + jnp.dot(p, stud_ref[cols, :], preferred_element_type=jnp.float32)

    acc = lax.fori_loop(
        0, blocks, step, jnp.zeros((tile, stud_ref.shape[1]), jnp.float32), unroll=blocks <= 4
    )
    out_ref[...] = acc.astype(jnp.bfloat16)


def pair_part(mask_sym, columns, student, group, block):
    n, dc = columns.shape
    p = student.shape[1]
    tile = block // 2
    blocks = n // block
    whole = lambda i: (0, 0)
    mine = lambda i: (i, 0)
    return pl.pallas_call(
        functools.partial(pair_kernel, block, blocks),
        grid=(n // tile,),
        in_specs=[
            pl.BlockSpec(memory_space=pltpu.SMEM),
            pl.BlockSpec((tile, dc), mine),
            pl.BlockSpec((n, dc), whole),
            pl.BlockSpec((n, p), whole),
            pl.BlockSpec((tile, 1), mine),
            pl.BlockSpec((1, n), whole),
        ],
        out_specs=pl.BlockSpec((tile, p), mine),
        out_shape=jax.ShapeDtypeStruct((n, p), jnp.bfloat16),
        compiler_params=pltpu.CompilerParams(vmem_limit_bytes=48 * 2**20),
        cost_estimate=pl.CostEstimate(
            flops=2 * n * n * (dc + p), bytes_accessed=2 * n * (dc + 2 * p), transcendentals=0
        ),
    )(mask_sym, columns, columns, student, group.reshape(n, 1), group.reshape(1, n))


def ring_kernel(
    wide, teacher, weight, mask, group, out,
    cols, stud, groups, far_out, far_in, grads,
    t_send, t_recv, g_send, g_recv, f_send, f_recv, s_send, s_recv, d_send, d_recv,
):
    rows, d = teacher.shape
    dc = cols.shape[1]
    count = wide * 4
    chips = count // 2
    w, nn = lax.axis_index("wide"), lax.axis_index("narrow")
    me = w * 4 + nn
    core = nn % 2
    chip = me // 2

    def at(i):
        return pl.ds(pl.multiple_of(i * rows, rows), rows)

    def dev(i):
        return {"wide": i // 4, "narrow": i % 4}

    def remote(source, target, send, recv, i):
        return pltpu.make_async_remote_copy(
            src_ref=source, dst_ref=target, send_sem=send, recv_sem=recv,
            device_id=dev(i), device_id_type=pl.DeviceIdType.MESH,
        )

    barrier = pltpu.get_barrier_semaphore()

    @pl.loop(1, count)
    def _(k):
        pl.semaphore_signal(
            barrier, inc=1, device_id=dev((me + k) % count), device_id_type=pl.DeviceIdType.MESH
        )

    pl.semaphore_wait(barrier, count - 1)

    def column_copy(peer, origin, k):
        part = pl.ds(pl.multiple_of(peer * dc, dc), dc)
        return remote(teacher.at[:, part], cols.at[at(origin), :], t_send.at[k], t_recv.at[k], peer)

    def group_copy(peer, origin, k):
        return remote(group.at[0], groups.at[origin], g_send.at[k], g_recv.at[k], peer)

    @pl.loop(1, count)
    def _(k):
        peer = (me + k) % count
        column_copy(peer, me, k).start()
        group_copy(peer, me, k).start()

    cols[at(me), :] = teacher[:, pl.ds(pl.multiple_of(me * dc, dc), dc)]
    groups[me] = group[0]

    step = 512

    def project(c, acc):
        part = pl.ds(pl.multiple_of(c * step, step), step)
        return acc + jnp.dot(
            teacher[:, part],
            weight[part, :].astype(jnp.bfloat16),
            preferred_element_type=jnp.float32,
        )

    own = lax.fori_loop(
        0, d // step, project, jnp.zeros((rows, stud.shape[1]), jnp.float32)
    )
    stud[at(me), :] = own.astype(jnp.bfloat16)

    def gather(buf, send, recv):
        nx = (nn + 2) % 4
        nc = nn + 1 - 2 * core
        ncx = (nc + 2) % 4

        def copy(origin_w, origin_n, slot, to):
            part = buf.at[at(origin_w * 4 + origin_n), :]
            return remote(part, part, send.at[slot], recv.at[slot], to)

        sent = []

        def go(*args):
            c = copy(*args)
            c.start()
            sent.append(c)

        a, b, c1, c2 = 0, wide, 2 * wide, 3 * wide
        for j in range(1, wide):
            go(w, nn, a + j, (w + j) % wide * 4 + nn)
        for j in range(wide):
            ow = (w + wide - j) % wide
            if j:
                copy(ow, nn, a + j, me).wait_recv()
            go(ow, nn, b + j, w * 4 + nx)
            go(ow, nn, c1 + j, w * 4 + nc)
        for j in range(wide):
            ow = (w + wide - j) % wide
            copy(ow, nx, b + j, me).wait_recv()
            go(ow, nx, c2 + j, w * 4 + nc)
        for j in range(wide):
            ow = (w + wide - j) % wide
            copy(ow, nc, c1 + j, me).wait_recv()
            copy(ow, ncx, c2 + j, me).wait_recv()
        for c in sent:
            c.wait_send()

    gather(stud, s_send, s_recv)

    @pl.loop(1, count)
    def _(k):
        origin = (me + count - k) % count
        column_copy(me, origin, k).wait_recv()
        group_copy(me, origin, k).wait_recv()

    def weights(gcol, b, f):
        return jnp.concatenate(
            [jnp.where(gcol == groups[b * 4 + i], 2.0 * f, f) for i in range(4)], axis=1
        )

    def spread(i):
        return jnp.broadcast_to(groups[i], (rows, rows)).T

    def terms(left, all_rows, gcol, mine, scale):
        acc = jnp.zeros((left.shape[0], stud.shape[1]), jnp.float32)
        for b in range(wide):
            span = pl.ds(b * 4 * rows, 4 * rows)
            e = lax.dot_general(left, all_rows[span, :], NT, preferred_element_type=jnp.float32)
            p = (e * weights(gcol, b, mask[mine, b] * scale)).astype(jnp.bfloat16)
            acc = acc + jnp.dot(p, stud[span, :], preferred_element_type=jnp.float32)
        return acc

    def far_rows(q):
        pair = pl.ds(pl.multiple_of(q * 2 * rows, 2 * rows), 2 * rows)
        gcol = jnp.concatenate([spread(2 * q), spread(2 * q + 1)], axis=0)
        far_out[pair, :] = terms(cols[pair, :], cols, gcol, q // 2, -1.0 / d).astype(jnp.bfloat16)

    def far_copy(peer, origin, s, r):
        return remote(far_out.at[at(peer), :], far_in.at[at(origin), :], f_send.at[s], f_recv.at[r], peer)

    partner = me + 1 - 2 * core

    @pl.loop(1, chips + 1)
    def _(k):
        q = (chip + k) % chips
        far_rows(q)

        @pl.when(k < chips)
        def _():
            for t in range(2):
                far_copy(2 * q + t, me, 2 * k + t, 2 * k + core).start()

    far_copy(partner, me, 0, core).start()

    width = stud.shape[1]
    total = terms(stud[at(me), :], stud, spread(me), w, 1.0 / width)
    total = total + far_out[at(me), :].astype(jnp.float32)
    far_copy(me, partner, 0, 1 - core).wait_recv()
    total = total + far_in[at(partner), :].astype(jnp.float32)

    def collect(k, total):
        for t in range(2):
            origin = 2 * ((chip + chips - k) % chips) + t
            far_copy(me, origin, 2 * k, 2 * k + t).wait_recv()
            total = total + far_in[at(origin), :].astype(jnp.float32)
        return total

    total = lax.fori_loop(1, chips, collect, total)
    grads[at(me), :] = (total * (2.0 * d / (rows * count * width))).astype(jnp.bfloat16)
    gather(grads, d_send, d_recv)
    acc = jnp.zeros(out.shape, jnp.float32)
    for b in range(wide):
        span = pl.ds(b * 4 * rows, 4 * rows)
        acc = acc + lax.dot_general(
            cols[span, :], grads[span, :], TN, preferred_element_type=jnp.float32
        )
    out[...] = acc

    @pl.loop(1, count)
    def _(k):
        peer = (me + k) % count
        column_copy(peer, me, k).wait_send()
        group_copy(peer, me, k).wait_send()

    @pl.loop(1, chips)
    def _(k):
        q = (chip + k) % chips
        for t in range(2):
            far_copy(2 * q + t, me, 2 * k + t, 2 * k + core).wait_send()

    far_copy(partner, me, 0, core).wait_send()


def in_one(teacher, weight, mask_sym, item_group, wide):
    rows, d = teacher.shape
    width = weight.shape[1]
    count = wide * 4
    n = rows * count
    dc = d // count
    vmem = pl.BlockSpec(memory_space=pltpu.VMEM)
    sem = pltpu.SemaphoreType.DMA
    return pl.pallas_call(
        functools.partial(ring_kernel, wide),
        in_specs=[vmem, vmem, pl.BlockSpec(memory_space=pltpu.SMEM), vmem],
        out_specs=vmem,
        out_shape=jax.ShapeDtypeStruct((dc, width), jnp.float32),
        scratch_shapes=[
            pltpu.VMEM((n, dc), jnp.bfloat16),
            pltpu.VMEM((n, width), jnp.bfloat16),
            pltpu.VMEM((count, 1, rows), jnp.float32),
            pltpu.VMEM((n, width), jnp.bfloat16),
            pltpu.VMEM((n, width), jnp.bfloat16),
            pltpu.VMEM((n, width), jnp.bfloat16),
        ]
        + [sem((count,))] * 6
        + [sem((4 * wide,))] * 4,
        compiler_params=pltpu.CompilerParams(
            collective_id=0, has_side_effects=True, vmem_limit_bytes=40 * 2**20
        ),
    )(teacher, weight, mask_sym, item_group.astype(jnp.float32).reshape(1, 1, rows))


def per_device(teacher, weight, block_mask, item_group):
    rows, d = teacher.shape
    width = weight.shape[1]
    wide = lax.axis_size("wide")
    count = wide * lax.axis_size("narrow")
    block = rows * lax.axis_size("narrow")
    n = rows * count
    here = lax.axis_index("wide")
    mask = block_mask.astype(jnp.float32)
    mask_sym = mask + mask.T
    if count == 4 * wide and d % (count * 128) == 0 and rows == 128 and n <= 2048:
        return in_one(teacher, weight, mask_sym, item_group, wide)
    columns = lax.all_to_all(teacher, AXES, split_axis=1, concat_axis=0, tiled=True)
    group = lax.all_gather(item_group, AXES, axis=0, tiled=True)
    own = jnp.dot(
        teacher, weight.astype(jnp.bfloat16), preferred_element_type=jnp.float32
    ).astype(jnp.bfloat16)
    student = lax.all_gather(own, AXES, axis=0, tiled=True)
    mine = lax.dynamic_index_in_dim(mask_sym, here, 0, keepdims=False)
    per_item = jnp.broadcast_to((mine / width)[:, None], (wide, block)).reshape(1, n)
    same = (item_group[:, None] == group[None, :]).astype(jnp.float32)
    stud = lax.dot_general(own, student, NT, preferred_element_type=jnp.float32)
    near = jnp.dot(
        (per_item * (1.0 + same) * stud).astype(jnp.bfloat16),
        student,
        preferred_element_type=jnp.float32,
    )
    far = pair_part(mask_sym * (-1.0 / d), columns, student, group, block)
    far = lax.all_to_all(far.reshape(count, rows, width), AXES, split_axis=0, concat_axis=0, tiled=True)
    total = near + jnp.sum(far.astype(jnp.float32), axis=0)
    grad = (total * (2.0 * d / (n * width))).astype(jnp.bfloat16)
    grad = lax.all_gather(grad, AXES, axis=0, tiled=True)
    return lax.dot_general(columns, grad, TN, preferred_element_type=jnp.float32)


def solution(mesh):
    in_specs = (P(("parts",) + AXES, None), P(), P("parts", None), P(("parts",) + AXES))
    return jax.shard_map(
        per_device,
        mesh=mesh,
        in_specs=in_specs,
        out_specs=P(("parts",) + AXES, None),
        check_vma=False,
    )
```

```python
import functools

import jax
import jax.numpy as jnp
from jax import lax
from jax.experimental import pallas as pl
from jax.experimental.pallas import tpu as pltpu
from jax.sharding import PartitionSpec as P

AXES = ("wide", "narrow")
NT = (((1,), (1,)), ((), ()))
TN = (((0,), (0,)), ((), ()))


def pair_kernel(block, blocks, mask_ref, rows_ref, all_ref, stud_ref, gcol_ref, grow_ref, out_ref):
    tile = rows_ref.shape[0]
    mine = pl.program_id(0) * tile // block
    rows = rows_ref[...]
    gcol = gcol_ref[...]

    def step(b, acc):
        cols = pl.ds(pl.multiple_of(b * block, block), block)
        e = lax.dot_general(rows, all_ref[cols, :], NT, preferred_element_type=jnp.float32)
        f = mask_ref[mine, b]
        w = jnp.where(gcol == grow_ref[:, cols], 2.0 * f, f)
        p = (e * w).astype(jnp.bfloat16)
        return acc + jnp.dot(p, stud_ref[cols, :], preferred_element_type=jnp.float32)

    acc = lax.fori_loop(
        0, blocks, step, jnp.zeros((tile, stud_ref.shape[1]), jnp.float32), unroll=blocks <= 4
    )
    out_ref[...] = acc.astype(jnp.bfloat16)


def pair_part(mask_sym, columns, student, group, block):
    n, dc = columns.shape
    p = student.shape[1]
    tile = block // 2
    blocks = n // block
    whole = lambda i: (0, 0)
    mine = lambda i: (i, 0)
    return pl.pallas_call(
        functools.partial(pair_kernel, block, blocks),
        grid=(n // tile,),
        in_specs=[
            pl.BlockSpec(memory_space=pltpu.SMEM),
            pl.BlockSpec((tile, dc), mine),
            pl.BlockSpec((n, dc), whole),
            pl.BlockSpec((n, p), whole),
            pl.BlockSpec((tile, 1), mine),
            pl.BlockSpec((1, n), whole),
        ],
        out_specs=pl.BlockSpec((tile, p), mine),
        out_shape=jax.ShapeDtypeStruct((n, p), jnp.bfloat16),
        compiler_params=pltpu.CompilerParams(vmem_limit_bytes=48 * 2**20),
        cost_estimate=pl.CostEstimate(
            flops=2 * n * n * (dc + p), bytes_accessed=2 * n * (dc + 2 * p), transcendentals=0
        ),
    )(mask_sym, columns, columns, student, group.reshape(n, 1), group.reshape(1, n))


def ring_kernel(
    wide, teacher_hbm, weight_hbm, mask, group, out,
    teacher, weight, cols, stud, groups, far_out, c_in, x_out, x_in, z_out, z_in, grads,
    t_send, t_recv, g_send, g_recv, c_send, c_recv, x_send, x_recv, z_send, z_recv,
    s_send, s_recv, d_send, d_recv, local,
):
    rows, d = teacher.shape
    loads = [
        pltpu.make_async_copy(teacher_hbm, teacher, local.at[0]),
        pltpu.make_async_copy(weight_hbm, weight, local.at[1]),
    ]
    for load in loads:
        load.start()
    dc = cols.shape[1]
    count = wide * 4
    w, nn = lax.axis_index("wide"), lax.axis_index("narrow")
    me = w * 4 + nn
    core = nn % 2

    def at(i):
        return pl.ds(pl.multiple_of(i * rows, rows), rows)

    def dev(i):
        return {"wide": i // 4, "narrow": i % 4}

    def remote(source, target, send, recv, i):
        return pltpu.make_async_remote_copy(
            src_ref=source, dst_ref=target, send_sem=send, recv_sem=recv,
            device_id=dev(i), device_id_type=pl.DeviceIdType.MESH,
        )

    barrier = pltpu.get_barrier_semaphore()

    @pl.loop(1, count)
    def _(k):
        pl.semaphore_signal(
            barrier, inc=1, device_id=dev((me + k) % count), device_id_type=pl.DeviceIdType.MESH
        )

    pl.semaphore_wait(barrier, count - 1)

    def column_copy(peer, origin, k):
        part = pl.ds(pl.multiple_of(peer * dc, dc), dc)
        return remote(teacher_hbm.at[:, part], cols.at[at(origin), :], t_send.at[k], t_recv.at[k], peer)

    def group_copy(peer, origin, k):
        return remote(group.at[0], groups.at[origin], g_send.at[k], g_recv.at[k], peer)

    @pl.loop(1, count)
    def _(k):
        peer = (me + k) % count
        column_copy(peer, me, k).start()
        group_copy(peer, me, k).start()

    for load in loads:
        load.wait()
    cols[at(me), :] = teacher[:, pl.ds(pl.multiple_of(me * dc, dc), dc)]
    groups[me] = group[0]

    step = 512

    def project(c, acc):
        part = pl.ds(pl.multiple_of(c * step, step), step)
        return acc + jnp.dot(
            teacher[:, part],
            weight[part, :].astype(jnp.bfloat16),
            preferred_element_type=jnp.float32,
        )

    own = lax.fori_loop(
        0, d // step, project, jnp.zeros((rows, stud.shape[1]), jnp.float32)
    )
    stud[at(me), :] = own.astype(jnp.bfloat16)

    def gather(buf, send, recv):
        nx = (nn + 2) % 4
        nc = nn + 1 - 2 * core
        ncx = (nc + 2) % 4

        def copy(origin_w, origin_n, slot, to):
            part = buf.at[at(origin_w * 4 + origin_n), :]
            return remote(part, part, send.at[slot], recv.at[slot], to)

        sent = []

        def go(*args):
            c = copy(*args)
            c.start()
            sent.append(c)

        a, b, c1, c2 = 0, wide, 2 * wide, 3 * wide
        for j in range(1, wide):
            go(w, nn, a + j, (w + j) % wide * 4 + nn)
        for j in range(wide):
            ow = (w + wide - j) % wide
            if j:
                copy(ow, nn, a + j, me).wait_recv()
            go(ow, nn, b + j, w * 4 + nx)
            go(ow, nn, c1 + j, w * 4 + nc)
        for j in range(wide):
            ow = (w + wide - j) % wide
            copy(ow, nx, b + j, me).wait_recv()
            go(ow, nx, c2 + j, w * 4 + nc)
        for j in range(wide):
            ow = (w + wide - j) % wide
            copy(ow, nc, c1 + j, me).wait_recv()
            copy(ow, ncx, c2 + j, me).wait_recv()
        for c in sent:
            c.wait_send()

    gather(stud, s_send, s_recv)

    @pl.loop(1, count)
    def _(k):
        origin = (me + count - k) % count
        column_copy(me, origin, k).wait_recv()
        group_copy(me, origin, k).wait_recv()

    def weights(gcol, b, f):
        return jnp.concatenate(
            [jnp.where(gcol == groups[b * 4 + i], 2.0 * f, f) for i in range(4)], axis=1
        )

    def spread(i):
        return jnp.broadcast_to(groups[i], (rows, rows)).T

    def terms(left, all_rows, gcol, mine, scale):
        acc = jnp.zeros((left.shape[0], stud.shape[1]), jnp.float32)
        for b in range(wide):
            span = pl.ds(b * 4 * rows, 4 * rows)
            e = lax.dot_general(left, all_rows[span, :], NT, preferred_element_type=jnp.float32)
            p = (e * weights(gcol, b, mask[mine, b] * scale)).astype(jnp.bfloat16)
            acc = acc + jnp.dot(p, stud[span, :], preferred_element_type=jnp.float32)
        return acc

    x = nn // 2
    other = 1 - core
    width = stud.shape[1]
    steps = [(j, 1 - x) for j in range(1, wide + 1)] + [(j, x) for j in range(1, wide + 1)]

    def slot(i):
        return pl.ds(i * rows, rows)

    def half(i, c):
        return pl.ds(pl.multiple_of((2 * i + c) * rows, rows), rows)

    def core_copy(i):
        return remote(
            far_out.at[half(i, other), :], c_in.at[slot(i), :],
            c_send.at[i], c_recv.at[i], w * 4 + nn + 1 - 2 * core,
        )

    def x_copy(j):
        return remote(
            x_out.at[slot(j - 1), :], x_in.at[slot(j - 1), :],
            x_send.at[j - 1], x_recv.at[j - 1], w * 4 + (nn + 2) % 4,
        )

    def z_copy(j):
        return remote(
            z_out.at[slot(j - 1), :], z_in.at[slot(j - 1), :],
            z_send.at[j - 1], z_recv.at[j - 1], (w + j) % wide * 4 + nn,
        )

    def compute(i):
        j, to_x = steps[i]
        q = (w + j) % wide * 2 + to_x
        pair = pl.ds(pl.multiple_of(q * 2 * rows, 2 * rows), 2 * rows)
        gcol = jnp.concatenate([spread(2 * q), spread(2 * q + 1)], axis=0)
        far_out[pl.ds(2 * i * rows, 2 * rows), :] = terms(
            cols[pair, :], cols, gcol, q // 2, -1.0 / d
        ).astype(jnp.bfloat16)
        core_copy(i).start()

    def finish(i):
        j, _ = steps[i]
        core_copy(i).wait_recv()
        part = far_out[half(i, core), :].astype(jnp.float32)
        part = part + c_in[slot(i), :].astype(jnp.float32)
        if i < wide:
            x_out[slot(j - 1), :] = part.astype(jnp.bfloat16)
            x_copy(j).start()
            return None
        x_copy(j).wait_recv()
        part = part + x_in[slot(j - 1), :].astype(jnp.float32)
        if j < wide:
            z_out[slot(j - 1), :] = part.astype(jnp.bfloat16)
            z_copy(j).start()
        return part

    for i in range(2 * wide):
        compute(i)
        if i:
            finish(i - 1)
    total = terms(stud[at(me), :], stud, spread(me), w, 1.0 / width)
    total = total + finish(2 * wide - 1)
    for j in range(1, wide):
        z_copy(j).wait_recv()
        total = total + z_in[slot(j - 1), :].astype(jnp.float32)
    grads[at(me), :] = (total * (2.0 * d / (rows * count * width))).astype(jnp.bfloat16)
    gather(grads, d_send, d_recv)
    acc = jnp.zeros(out.shape, jnp.float32)
    for b in range(wide):
        span = pl.ds(b * 4 * rows, 4 * rows)
        acc = acc + lax.dot_general(
            cols[span, :], grads[span, :], TN, preferred_element_type=jnp.float32
        )
    out[...] = acc

    @pl.loop(1, count)
    def _(k):
        peer = (me + k) % count
        column_copy(peer, me, k).wait_send()
        group_copy(peer, me, k).wait_send()

    for i in range(2 * wide):
        core_copy(i).wait_send()
    for j in range(1, wide + 1):
        x_copy(j).wait_send()
    for j in range(1, wide):
        z_copy(j).wait_send()


def in_one(teacher, weight, mask_sym, item_group, wide):
    rows, d = teacher.shape
    width = weight.shape[1]
    count = wide * 4
    n = rows * count
    dc = d // count
    vmem = pl.BlockSpec(memory_space=pltpu.VMEM)
    hbm = pl.BlockSpec(memory_space=pltpu.HBM)
    sem = pltpu.SemaphoreType.DMA
    return pl.pallas_call(
        functools.partial(ring_kernel, wide),
        in_specs=[hbm, hbm, pl.BlockSpec(memory_space=pltpu.SMEM), vmem],
        out_specs=vmem,
        out_shape=jax.ShapeDtypeStruct((dc, width), jnp.float32),
        scratch_shapes=[
            pltpu.VMEM((rows, d), jnp.bfloat16),
            pltpu.VMEM((d, width), jnp.float32),
            pltpu.VMEM((n, dc), jnp.bfloat16),
            pltpu.VMEM((n, width), jnp.bfloat16),
            pltpu.VMEM((count, 1, rows), jnp.float32),
            pltpu.VMEM((n, width), jnp.bfloat16),
            pltpu.VMEM((2 * wide * rows, width), jnp.bfloat16),
        ]
        + [pltpu.VMEM((wide * rows, width), jnp.bfloat16)] * 4
        + [pltpu.VMEM((n, width), jnp.bfloat16)]
        + [sem((count,))] * 4
        + [sem((2 * wide,))] * 2
        + [sem((wide,))] * 4
        + [sem((4 * wide,))] * 4
        + [sem((2,))],
        compiler_params=pltpu.CompilerParams(
            collective_id=0, has_side_effects=True, vmem_limit_bytes=40 * 2**20
        ),
    )(teacher, weight, mask_sym, item_group.astype(jnp.float32).reshape(1, 1, rows))


def per_device(teacher, weight, block_mask, item_group):
    rows, d = teacher.shape
    width = weight.shape[1]
    wide = lax.axis_size("wide")
    count = wide * lax.axis_size("narrow")
    block = rows * lax.axis_size("narrow")
    n = rows * count
    here = lax.axis_index("wide")
    mask = block_mask.astype(jnp.float32)
    mask_sym = mask + mask.T
    if count == 4 * wide and d % (count * 128) == 0 and rows == 128 and n <= 2048:
        return in_one(teacher, weight, mask_sym, item_group, wide)
    columns = lax.all_to_all(teacher, AXES, split_axis=1, concat_axis=0, tiled=True)
    group = lax.all_gather(item_group, AXES, axis=0, tiled=True)
    own = jnp.dot(
        teacher, weight.astype(jnp.bfloat16), preferred_element_type=jnp.float32
    ).astype(jnp.bfloat16)
    student = lax.all_gather(own, AXES, axis=0, tiled=True)
    mine = lax.dynamic_index_in_dim(mask_sym, here, 0, keepdims=False)
    per_item = jnp.broadcast_to((mine / width)[:, None], (wide, block)).reshape(1, n)
    same = (item_group[:, None] == group[None, :]).astype(jnp.float32)
    stud = lax.dot_general(own, student, NT, preferred_element_type=jnp.float32)
    near = jnp.dot(
        (per_item * (1.0 + same) * stud).astype(jnp.bfloat16),
        student,
        preferred_element_type=jnp.float32,
    )
    far = pair_part(mask_sym * (-1.0 / d), columns, student, group, block)
    far = lax.all_to_all(far.reshape(count, rows, width), AXES, split_axis=0, concat_axis=0, tiled=True)
    total = near + jnp.sum(far.astype(jnp.float32), axis=0)
    grad = (total * (2.0 * d / (n * width))).astype(jnp.bfloat16)
    grad = lax.all_gather(grad, AXES, axis=0, tiled=True)
    return lax.dot_general(columns, grad, TN, preferred_element_type=jnp.float32)


def solution(mesh):
    in_specs = (P(("parts",) + AXES, None), P(), P("parts", None), P(("parts",) + AXES))
    return jax.shard_map(
        per_device,
        mesh=mesh,
        in_specs=in_specs,
        out_specs=P(("parts",) + AXES, None),
        check_vma=False,
    )
```

```python
import functools

import jax
import jax.numpy as jnp
from jax import lax
from jax.experimental import pallas as pl
from jax.experimental.pallas import tpu as pltpu
from jax.sharding import PartitionSpec as P

AXES = ("wide", "narrow")
NT = (((1,), (1,)), ((), ()))
TN = (((0,), (0,)), ((), ()))


def pair_kernel(block, blocks, mask_ref, rows_ref, all_ref, stud_ref, gcol_ref, grow_ref, out_ref):
    tile = rows_ref.shape[0]
    mine = pl.program_id(0) * tile // block
    rows = rows_ref[...]
    gcol = gcol_ref[...]

    def step(b, acc):
        cols = pl.ds(pl.multiple_of(b * block, block), block)
        e = lax.dot_general(rows, all_ref[cols, :], NT, preferred_element_type=jnp.float32)
        f = mask_ref[mine, b]
        w = jnp.where(gcol == grow_ref[:, cols], 2.0 * f, f)
        p = (e * w).astype(jnp.bfloat16)
        return acc + jnp.dot(p, stud_ref[cols, :], preferred_element_type=jnp.float32)

    acc = lax.fori_loop(
        0, blocks, step, jnp.zeros((tile, stud_ref.shape[1]), jnp.float32), unroll=blocks <= 4
    )
    out_ref[...] = acc.astype(jnp.bfloat16)


def pair_part(mask_sym, columns, student, group, block):
    n, dc = columns.shape
    p = student.shape[1]
    tile = block // 2
    blocks = n // block
    whole = lambda i: (0, 0)
    mine = lambda i: (i, 0)
    return pl.pallas_call(
        functools.partial(pair_kernel, block, blocks),
        grid=(n // tile,),
        in_specs=[
            pl.BlockSpec(memory_space=pltpu.SMEM),
            pl.BlockSpec((tile, dc), mine),
            pl.BlockSpec((n, dc), whole),
            pl.BlockSpec((n, p), whole),
            pl.BlockSpec((tile, 1), mine),
            pl.BlockSpec((1, n), whole),
        ],
        out_specs=pl.BlockSpec((tile, p), mine),
        out_shape=jax.ShapeDtypeStruct((n, p), jnp.bfloat16),
        compiler_params=pltpu.CompilerParams(vmem_limit_bytes=48 * 2**20),
        cost_estimate=pl.CostEstimate(
            flops=2 * n * n * (dc + p), bytes_accessed=2 * n * (dc + 2 * p), transcendentals=0
        ),
    )(mask_sym, columns, columns, student, group.reshape(n, 1), group.reshape(1, n))


def ring_kernel(
    wide, teacher_hbm, weight_hbm, mask, group, out,
    teacher, weight, cols, stud, groups, far_out, c_in, x_out, x_in, z_out, z_in, grads, flipped,
    t_send, t_recv, g_send, g_recv, c_send, c_recv, x_send, x_recv, z_send, z_recv,
    s_send, s_recv, d_send, d_recv, local,
):
    rows, d = teacher.shape
    loads = [
        pltpu.make_async_copy(teacher_hbm, teacher, local.at[0]),
        pltpu.make_async_copy(weight_hbm, weight, local.at[1]),
    ]
    for load in loads:
        load.start()
    dc = cols.shape[1]
    count = wide * 4
    w, nn = lax.axis_index("wide"), lax.axis_index("narrow")
    me = w * 4 + nn
    core = nn % 2

    def at(i):
        return pl.ds(pl.multiple_of(i * rows, rows), rows)

    def dev(i):
        return {"wide": i // 4, "narrow": i % 4}

    def remote(source, target, send, recv, i):
        return pltpu.make_async_remote_copy(
            src_ref=source, dst_ref=target, send_sem=send, recv_sem=recv,
            device_id=dev(i), device_id_type=pl.DeviceIdType.MESH,
        )

    barrier = pltpu.get_barrier_semaphore()

    @pl.loop(1, count)
    def _(k):
        pl.semaphore_signal(
            barrier, inc=1, device_id=dev((me + k) % count), device_id_type=pl.DeviceIdType.MESH
        )

    pl.semaphore_wait(barrier, count - 1)

    def column_copy(peer, origin, k):
        part = pl.ds(pl.multiple_of(peer * dc, dc), dc)
        return remote(teacher_hbm.at[:, part], cols.at[at(origin), :], t_send.at[k], t_recv.at[k], peer)

    def group_copy(peer, origin, k):
        return remote(group.at[0], groups.at[origin], g_send.at[k], g_recv.at[k], peer)

    @pl.loop(1, count)
    def _(k):
        peer = (me + k) % count
        column_copy(peer, me, k).start()
        group_copy(peer, me, k).start()

    for load in loads:
        load.wait()
    cols[at(me), :] = teacher[:, pl.ds(pl.multiple_of(me * dc, dc), dc)]
    groups[me] = group[0]

    step = 512

    def project(c, acc):
        part = pl.ds(pl.multiple_of(c * step, step), step)
        return acc + jnp.dot(
            teacher[:, part],
            weight[part, :].astype(jnp.bfloat16),
            preferred_element_type=jnp.float32,
        )

    own = lax.fori_loop(
        0, d // step, project, jnp.zeros((rows, stud.shape[1]), jnp.float32)
    )
    stud[at(me), :] = own.astype(jnp.bfloat16)

    def gather(buf, send, recv, use):
        nx = (nn + 2) % 4
        nc = nn + 1 - 2 * core
        ncx = (nc + 2) % 4

        def copy(origin_w, origin_n, slot, to):
            part = buf.at[at(origin_w * 4 + origin_n), :]
            return remote(part, part, send.at[slot], recv.at[slot], to)

        sent = []

        def go(*args):
            c = copy(*args)
            c.start()
            sent.append(c)

        def landed(*args):
            copy(*args, me).wait_recv()

        a, b, c1, c2 = 0, wide, 2 * wide, 3 * wide
        planes = [w, w + 1 - 2 * (w % 2), (w + 2) % 4, 3 - w]
        for j in (3, 2, 1):
            go(w, nn, a + j, planes[j] * 4 + nn)
        go(w, nn, b, w * 4 + nx)
        go(w, nn, c1, w * 4 + nc)
        landed(w, nx, b)
        go(w, nx, c2, w * 4 + nc)
        for j in range(1, wide):
            landed(planes[j], nn, a + j)
            go(planes[j], nn, b + j, w * 4 + nx)
            go(planes[j], nn, c1 + j, w * 4 + nc)
            if j == 1:
                landed(w, nc, c1)
                landed(w, ncx, c2)
                use(w)
        for j in range(1, wide):
            landed(planes[j], nx, b + j)
            go(planes[j], nx, c2 + j, w * 4 + nc)
        for j in range(1, wide):
            landed(planes[j], nc, c1 + j)
            landed(planes[j], ncx, c2 + j)
            use(planes[j])
        for c in sent:
            c.wait_send()

    gather(stud, s_send, s_recv, lambda plane: None)

    @pl.loop(1, count)
    def _(k):
        origin = (me + count - k) % count
        column_copy(me, origin, k).wait_recv()
        group_copy(me, origin, k).wait_recv()

    def weights(gcol, b, f):
        return jnp.concatenate(
            [jnp.where(gcol == groups[b * 4 + i].astype(jnp.float32), 2.0 * f, f) for i in range(4)], axis=1
        )

    def spread(i):
        return jnp.broadcast_to(groups[i].astype(jnp.float32), (rows, rows)).T

    def terms(left, all_rows, gcol, mine, scale):
        acc = jnp.zeros((left.shape[0], stud.shape[1]), jnp.float32)
        for b in range(wide):
            span = pl.ds(b * 4 * rows, 4 * rows)
            e = lax.dot_general(left, all_rows[span, :], NT, preferred_element_type=jnp.float32)
            f = (mask[mine, b] + mask[b, mine]).astype(jnp.float32) * scale
            p = (e * weights(gcol, b, f)).astype(jnp.bfloat16)
            acc = acc + jnp.dot(p, stud[span, :], preferred_element_type=jnp.float32)
        return acc

    x = nn // 2
    other = 1 - core
    width = stud.shape[1]
    steps = [(j, 1 - x) for j in range(1, wide + 1)] + [(j, x) for j in range(1, wide + 1)]

    def slot(i):
        return pl.ds(i * rows, rows)

    def half(i, c):
        return pl.ds(pl.multiple_of((2 * i + c) * rows, rows), rows)

    def core_copy(i):
        return remote(
            far_out.at[half(i, other), :], c_in.at[slot(i), :],
            c_send.at[i], c_recv.at[i], w * 4 + nn + 1 - 2 * core,
        )

    def x_copy(j):
        return remote(
            x_out.at[slot(j - 1), :], x_in.at[slot(j - 1), :],
            x_send.at[j - 1], x_recv.at[j - 1], w * 4 + (nn + 2) % 4,
        )

    def z_copy(j):
        return remote(
            z_out.at[slot(j - 1), :], z_in.at[slot(j - 1), :],
            z_send.at[j - 1], z_recv.at[j - 1], (w + j) % wide * 4 + nn,
        )

    def compute(i):
        j, to_x = steps[i]
        q = (w + j) % wide * 2 + to_x
        pair = pl.ds(pl.multiple_of(q * 2 * rows, 2 * rows), 2 * rows)
        gcol = jnp.concatenate([spread(2 * q), spread(2 * q + 1)], axis=0)
        far_out[pl.ds(2 * i * rows, 2 * rows), :] = terms(
            cols[pair, :], cols, gcol, q // 2, -1.0 / d
        ).astype(jnp.bfloat16)
        core_copy(i).start()

    def finish(i):
        j, _ = steps[i]
        core_copy(i).wait_recv()
        part = far_out[half(i, core), :].astype(jnp.float32)
        part = part + c_in[slot(i), :].astype(jnp.float32)
        if i < wide:
            x_out[slot(j - 1), :] = part.astype(jnp.bfloat16)
            x_copy(j).start()
            return None
        x_copy(j).wait_recv()
        part = part + x_in[slot(j - 1), :].astype(jnp.float32)
        if j < wide:
            z_out[slot(j - 1), :] = part.astype(jnp.bfloat16)
            z_copy(j).start()
        return part

    for i in range(2 * wide):
        compute(i)
        if i:
            finish(i - 1)
    total = terms(stud[at(me), :], stud, spread(me), w, 1.0 / width)
    total = total + finish(2 * wide - 1)
    for b in range(wide):
        span = pl.ds(b * 4 * rows, 4 * rows)
        flipped[:, span] = cols[span, :].T
    for j in range(1, wide):
        z_copy(j).wait_recv()
        total = total + z_in[slot(j - 1), :].astype(jnp.float32)
    grads[at(me), :] = (total * (2.0 * d / (rows * count * width))).astype(jnp.bfloat16)
    out[...] = jnp.zeros_like(out)

    def use(plane):
        span = pl.ds(pl.multiple_of(plane * 4 * rows, 4 * rows), 4 * rows)
        out[...] += jnp.dot(flipped[:, span], grads[span, :], preferred_element_type=jnp.float32)

    gather(grads, d_send, d_recv, use)

    @pl.loop(1, count)
    def _(k):
        peer = (me + k) % count
        column_copy(peer, me, k).wait_send()
        group_copy(peer, me, k).wait_send()

    for i in range(2 * wide):
        core_copy(i).wait_send()
    for j in range(1, wide + 1):
        x_copy(j).wait_send()
    for j in range(1, wide):
        z_copy(j).wait_send()


def in_one(teacher, weight, block_mask, item_group, wide):
    rows, d = teacher.shape
    width = weight.shape[1]
    count = wide * 4
    n = rows * count
    dc = d // count
    vmem = pl.BlockSpec(memory_space=pltpu.VMEM)
    hbm = pl.BlockSpec(memory_space=pltpu.HBM)
    sem = pltpu.SemaphoreType.DMA
    return pl.pallas_call(
        functools.partial(ring_kernel, wide),
        in_specs=[hbm, hbm, pl.BlockSpec(memory_space=pltpu.SMEM), vmem],
        out_specs=vmem,
        out_shape=jax.ShapeDtypeStruct((dc, width), jnp.float32),
        scratch_shapes=[
            pltpu.VMEM((rows, d), jnp.bfloat16),
            pltpu.VMEM((d, width), jnp.float32),
            pltpu.VMEM((n, dc), jnp.bfloat16),
            pltpu.VMEM((n, width), jnp.bfloat16),
            pltpu.VMEM((count, 1, rows), jnp.int32),
            pltpu.VMEM((n, width), jnp.bfloat16),
            pltpu.VMEM((2 * wide * rows, width), jnp.bfloat16),
        ]
        + [pltpu.VMEM((wide * rows, width), jnp.bfloat16)] * 4
        + [pltpu.VMEM((n, width), jnp.bfloat16), pltpu.VMEM((dc, n), jnp.bfloat16)]
        + [sem((count,))] * 4
        + [sem((2 * wide,))] * 2
        + [sem((wide,))] * 4
        + [sem((4 * wide,))] * 4
        + [sem((2,))],
        compiler_params=pltpu.CompilerParams(
            collective_id=0, has_side_effects=True, vmem_limit_bytes=62 * 2**20
        ),
    )(teacher, weight, block_mask, item_group.reshape(1, 1, rows))


def per_device(teacher, weight, block_mask, item_group):
    rows, d = teacher.shape
    width = weight.shape[1]
    wide = lax.axis_size("wide")
    count = wide * lax.axis_size("narrow")
    block = rows * lax.axis_size("narrow")
    n = rows * count
    here = lax.axis_index("wide")
    mask = block_mask.astype(jnp.float32)
    mask_sym = mask + mask.T
    if count == 4 * wide and wide == 4 and d % (count * 128) == 0 and rows == 128 and n <= 2048:
        return in_one(teacher, weight, block_mask, item_group, wide)
    columns = lax.all_to_all(teacher, AXES, split_axis=1, concat_axis=0, tiled=True)
    group = lax.all_gather(item_group, AXES, axis=0, tiled=True)
    own = jnp.dot(
        teacher, weight.astype(jnp.bfloat16), preferred_element_type=jnp.float32
    ).astype(jnp.bfloat16)
    student = lax.all_gather(own, AXES, axis=0, tiled=True)
    mine = lax.dynamic_index_in_dim(mask_sym, here, 0, keepdims=False)
    per_item = jnp.broadcast_to((mine / width)[:, None], (wide, block)).reshape(1, n)
    same = (item_group[:, None] == group[None, :]).astype(jnp.float32)
    stud = lax.dot_general(own, student, NT, preferred_element_type=jnp.float32)
    near = jnp.dot(
        (per_item * (1.0 + same) * stud).astype(jnp.bfloat16),
        student,
        preferred_element_type=jnp.float32,
    )
    far = pair_part(mask_sym * (-1.0 / d), columns, student, group, block)
    far = lax.all_to_all(far.reshape(count, rows, width), AXES, split_axis=0, concat_axis=0, tiled=True)
    total = near + jnp.sum(far.astype(jnp.float32), axis=0)
    grad = (total * (2.0 * d / (n * width))).astype(jnp.bfloat16)
    grad = lax.all_gather(grad, AXES, axis=0, tiled=True)
    return lax.dot_general(columns, grad, TN, preferred_element_type=jnp.float32)


def solution(mesh):
    in_specs = (P(("parts",) + AXES, None), P(), P("parts", None), P(("parts",) + AXES))
    return jax.shard_map(
        per_device,
        mesh=mesh,
        in_specs=in_specs,
        out_specs=P(("parts",) + AXES, None),
        check_vma=False,
    )
```

```python
import functools

import jax
import jax.numpy as jnp
from jax import lax
from jax.experimental import pallas as pl
from jax.experimental.pallas import tpu as pltpu
from jax.sharding import PartitionSpec as P

AXES = ("wide", "narrow")
NT = (((1,), (1,)), ((), ()))
TN = (((0,), (0,)), ((), ()))


def pair_kernel(block, blocks, mask_ref, rows_ref, all_ref, stud_ref, gcol_ref, grow_ref, out_ref):
    tile = rows_ref.shape[0]
    mine = pl.program_id(0) * tile // block
    rows = rows_ref[...]
    gcol = gcol_ref[...]

    def step(b, acc):
        cols = pl.ds(pl.multiple_of(b * block, block), block)
        e = lax.dot_general(rows, all_ref[cols, :], NT, preferred_element_type=jnp.float32)
        f = mask_ref[mine, b]
        w = jnp.where(gcol == grow_ref[:, cols], 2.0 * f, f)
        p = (e * w).astype(jnp.bfloat16)
        return acc + jnp.dot(p, stud_ref[cols, :], preferred_element_type=jnp.float32)

    acc = lax.fori_loop(
        0, blocks, step, jnp.zeros((tile, stud_ref.shape[1]), jnp.float32), unroll=blocks <= 4
    )
    out_ref[...] = acc.astype(jnp.bfloat16)


def pair_part(mask_sym, columns, student, group, block):
    n, dc = columns.shape
    p = student.shape[1]
    tile = block // 2
    blocks = n // block
    whole = lambda i: (0, 0)
    mine = lambda i: (i, 0)
    return pl.pallas_call(
        functools.partial(pair_kernel, block, blocks),
        grid=(n // tile,),
        in_specs=[
            pl.BlockSpec(memory_space=pltpu.SMEM),
            pl.BlockSpec((tile, dc), mine),
            pl.BlockSpec((n, dc), whole),
            pl.BlockSpec((n, p), whole),
            pl.BlockSpec((tile, 1), mine),
            pl.BlockSpec((1, n), whole),
        ],
        out_specs=pl.BlockSpec((tile, p), mine),
        out_shape=jax.ShapeDtypeStruct((n, p), jnp.bfloat16),
        compiler_params=pltpu.CompilerParams(vmem_limit_bytes=48 * 2**20),
        cost_estimate=pl.CostEstimate(
            flops=2 * n * n * (dc + p), bytes_accessed=2 * n * (dc + 2 * p), transcendentals=0
        ),
    )(mask_sym, columns, columns, student, group.reshape(n, 1), group.reshape(1, n))


def ring_kernel(
    wide, teacher_hbm, weight_hbm, mask, group, out,
    teacher, weight, cols, stud, groups, far_out, c_in, x_out, x_in, z_out, z_in, grads, flipped,
    t_send, t_recv, g_send, g_recv, c_send, c_recv, x_send, x_recv, z_send, z_recv,
    s_send, s_recv, d_send, d_recv, local,
):
    rows, d = teacher.shape
    loads = [
        pltpu.make_async_copy(teacher_hbm, teacher, local.at[0]),
        pltpu.make_async_copy(weight_hbm, weight, local.at[1]),
    ]
    for load in loads:
        load.start()
    dc = cols.shape[1]
    count = wide * 4
    w, nn = lax.axis_index("wide"), lax.axis_index("narrow")
    me = w * 4 + nn
    core = nn % 2

    def at(i):
        return pl.ds(pl.multiple_of(i * rows, rows), rows)

    def dev(i):
        return {"wide": i // 4, "narrow": i % 4}

    def remote(source, target, send, recv, i):
        return pltpu.make_async_remote_copy(
            src_ref=source, dst_ref=target, send_sem=send, recv_sem=recv,
            device_id=dev(i), device_id_type=pl.DeviceIdType.MESH,
        )

    barrier = pltpu.get_barrier_semaphore()

    @pl.loop(1, count)
    def _(k):
        pl.semaphore_signal(
            barrier, inc=1, device_id=dev((me + k) % count), device_id_type=pl.DeviceIdType.MESH
        )

    pl.semaphore_wait(barrier, count - 1)

    def column_copy(peer, origin, k):
        part = pl.ds(pl.multiple_of(peer * dc, dc), dc)
        return remote(teacher_hbm.at[:, part], cols.at[at(origin), :], t_send.at[k], t_recv.at[k], peer)

    def group_copy(peer, origin, k):
        return remote(group.at[0], groups.at[origin], g_send.at[k], g_recv.at[k], peer)

    @pl.loop(1, count)
    def _(k):
        group_copy((me + k) % count, me, k).start()

    def send_columns(first, last):
        @pl.loop(first, last)
        def _(i):
            k = 1 + (i + 6) % (count - 1)
            column_copy((me + k) % count, me, k).start()

    send_columns(0, 5)

    for load in loads:
        load.wait()
    cols[at(me), :] = teacher[:, pl.ds(pl.multiple_of(me * dc, dc), dc)]
    groups[me] = group[0]

    step = 512

    def project(c, acc):
        part = pl.ds(pl.multiple_of(c * step, step), step)
        return acc + jnp.dot(
            teacher[:, part],
            weight[part, :].astype(jnp.bfloat16),
            preferred_element_type=jnp.float32,
        )

    own = lax.fori_loop(
        0, d // step, project, jnp.zeros((rows, stud.shape[1]), jnp.float32)
    )
    stud[at(me), :] = own.astype(jnp.bfloat16)

    def gather(buf, send, recv, use, then):
        nx = (nn + 2) % 4
        nc = nn + 1 - 2 * core
        ncx = (nc + 2) % 4

        def copy(origin_w, origin_n, slot, to):
            part = buf.at[at(origin_w * 4 + origin_n), :]
            return remote(part, part, send.at[slot], recv.at[slot], to)

        sent = []

        def go(*args):
            c = copy(*args)
            c.start()
            sent.append(c)

        def landed(*args):
            copy(*args, me).wait_recv()

        a, b, c1, c2 = 0, wide, 2 * wide, 3 * wide
        planes = [w, w + 1 - 2 * (w % 2), (w + 2) % 4, 3 - w]
        for j in (3, 2, 1):
            go(w, nn, a + j, planes[j] * 4 + nn)
        go(w, nn, b, w * 4 + nx)
        go(w, nn, c1, w * 4 + nc)
        then()
        landed(w, nx, b)
        go(w, nx, c2, w * 4 + nc)
        for j in range(1, wide):
            landed(planes[j], nn, a + j)
            go(planes[j], nn, b + j, w * 4 + nx)
            go(planes[j], nn, c1 + j, w * 4 + nc)
            if j == 1:
                landed(w, nc, c1)
                landed(w, ncx, c2)
                use(w)
        for j in range(1, wide):
            landed(planes[j], nx, b + j)
            go(planes[j], nx, c2 + j, w * 4 + nc)
        for j in range(1, wide):
            landed(planes[j], nc, c1 + j)
            landed(planes[j], ncx, c2 + j)
            use(planes[j])
        for c in sent:
            c.wait_send()

    gather(stud, s_send, s_recv, lambda plane: None, lambda: send_columns(5, count - 1))

    @pl.loop(1, count)
    def _(k):
        origin = (me + count - k) % count
        column_copy(me, origin, k).wait_recv()
        group_copy(me, origin, k).wait_recv()

    def weights(gcol, b, f):
        return jnp.concatenate(
            [jnp.where(gcol == groups[b * 4 + i].astype(jnp.float32), 2.0 * f, f) for i in range(4)], axis=1
        )

    def spread(i):
        return jnp.broadcast_to(groups[i].astype(jnp.float32), (rows, rows)).T

    def terms(left, all_rows, gcol, mine, scale):
        acc = jnp.zeros((left.shape[0], stud.shape[1]), jnp.float32)
        for b in range(wide):
            span = pl.ds(b * 4 * rows, 4 * rows)
            e = lax.dot_general(left, all_rows[span, :], NT, preferred_element_type=jnp.float32)
            f = (mask[mine, b] + mask[b, mine]).astype(jnp.float32) * scale
            p = (e * weights(gcol, b, f)).astype(jnp.bfloat16)
            acc = acc + jnp.dot(p, stud[span, :], preferred_element_type=jnp.float32)
        return acc

    x = nn // 2
    other = 1 - core
    width = stud.shape[1]
    steps = [(j, 1 - x) for j in range(1, wide + 1)] + [(j, x) for j in range(1, wide + 1)]

    def slot(i):
        return pl.ds(i * rows, rows)

    def half(i, c):
        return pl.ds(pl.multiple_of((2 * i + c) * rows, rows), rows)

    def core_copy(i):
        return remote(
            far_out.at[half(i, other), :], c_in.at[slot(i), :],
            c_send.at[i], c_recv.at[i], w * 4 + nn + 1 - 2 * core,
        )

    def x_copy(j):
        return remote(
            x_out.at[slot(j - 1), :], x_in.at[slot(j - 1), :],
            x_send.at[j - 1], x_recv.at[j - 1], w * 4 + (nn + 2) % 4,
        )

    def z_copy(j):
        return remote(
            z_out.at[slot(j - 1), :], z_in.at[slot(j - 1), :],
            z_send.at[j - 1], z_recv.at[j - 1], (w + j) % wide * 4 + nn,
        )

    def compute(i):
        j, to_x = steps[i]
        q = (w + j) % wide * 2 + to_x
        pair = pl.ds(pl.multiple_of(q * 2 * rows, 2 * rows), 2 * rows)
        gcol = jnp.concatenate([spread(2 * q), spread(2 * q + 1)], axis=0)
        far_out[pl.ds(2 * i * rows, 2 * rows), :] = terms(
            cols[pair, :], cols, gcol, q // 2, -1.0 / d
        ).astype(jnp.bfloat16)
        core_copy(i).start()

    def finish(i):
        j, _ = steps[i]
        core_copy(i).wait_recv()
        part = far_out[half(i, core), :].astype(jnp.float32)
        part = part + c_in[slot(i), :].astype(jnp.float32)
        if i < wide:
            x_out[slot(j - 1), :] = part.astype(jnp.bfloat16)
            x_copy(j).start()
            return None
        x_copy(j).wait_recv()
        part = part + x_in[slot(j - 1), :].astype(jnp.float32)
        if j < wide:
            z_out[slot(j - 1), :] = part.astype(jnp.bfloat16)
            z_copy(j).start()
        return part

    for i in range(2 * wide):
        compute(i)
        if i:
            finish(i - 1)
    total = terms(stud[at(me), :], stud, spread(me), w, 1.0 / width)
    total = total + finish(2 * wide - 1)
    for b in range(wide):
        span = pl.ds(b * 4 * rows, 4 * rows)
        flipped[:, span] = cols[span, :].T
    for j in range(1, wide):
        z_copy(j).wait_recv()
        total = total + z_in[slot(j - 1), :].astype(jnp.float32)
    grads[at(me), :] = (total * (2.0 * d / (rows * count * width))).astype(jnp.bfloat16)
    out[...] = jnp.zeros_like(out)

    def use(plane):
        span = pl.ds(pl.multiple_of(plane * 4 * rows, 4 * rows), 4 * rows)
        out[...] += jnp.dot(flipped[:, span], grads[span, :], preferred_element_type=jnp.float32)

    gather(grads, d_send, d_recv, use, lambda: None)

    @pl.loop(1, count)
    def _(k):
        peer = (me + k) % count
        column_copy(peer, me, k).wait_send()
        group_copy(peer, me, k).wait_send()

    for i in range(2 * wide):
        core_copy(i).wait_send()
    for j in range(1, wide + 1):
        x_copy(j).wait_send()
    for j in range(1, wide):
        z_copy(j).wait_send()


def in_one(teacher, weight, block_mask, item_group, wide):
    rows, d = teacher.shape
    width = weight.shape[1]
    count = wide * 4
    n = rows * count
    dc = d // count
    vmem = pl.BlockSpec(memory_space=pltpu.VMEM)
    hbm = pl.BlockSpec(memory_space=pltpu.HBM)
    sem = pltpu.SemaphoreType.DMA
    return pl.pallas_call(
        functools.partial(ring_kernel, wide),
        in_specs=[hbm, hbm, pl.BlockSpec(memory_space=pltpu.SMEM), vmem],
        out_specs=vmem,
        out_shape=jax.ShapeDtypeStruct((dc, width), jnp.float32),
        scratch_shapes=[
            pltpu.VMEM((rows, d), jnp.bfloat16),
            pltpu.VMEM((d, width), jnp.float32),
            pltpu.VMEM((n, dc), jnp.bfloat16),
            pltpu.VMEM((n, width), jnp.bfloat16),
            pltpu.VMEM((count, 1, rows), jnp.int32),
            pltpu.VMEM((n, width), jnp.bfloat16),
            pltpu.VMEM((2 * wide * rows, width), jnp.bfloat16),
        ]
        + [pltpu.VMEM((wide * rows, width), jnp.bfloat16)] * 4
        + [pltpu.VMEM((n, width), jnp.bfloat16), pltpu.VMEM((dc, n), jnp.bfloat16)]
        + [sem((count,))] * 4
        + [sem((2 * wide,))] * 2
        + [sem((wide,))] * 4
        + [sem((4 * wide,))] * 4
        + [sem((2,))],
        compiler_params=pltpu.CompilerParams(
            collective_id=0, has_side_effects=True, vmem_limit_bytes=62 * 2**20
        ),
    )(teacher, weight, block_mask, item_group.reshape(1, 1, rows))


def per_device(teacher, weight, block_mask, item_group):
    rows, d = teacher.shape
    width = weight.shape[1]
    wide = lax.axis_size("wide")
    count = wide * lax.axis_size("narrow")
    block = rows * lax.axis_size("narrow")
    n = rows * count
    here = lax.axis_index("wide")
    mask = block_mask.astype(jnp.float32)
    mask_sym = mask + mask.T
    if count == 4 * wide and wide == 4 and d % (count * 128) == 0 and rows == 128 and n <= 2048:
        return in_one(teacher, weight, block_mask, item_group, wide)
    columns = lax.all_to_all(teacher, AXES, split_axis=1, concat_axis=0, tiled=True)
    group = lax.all_gather(item_group, AXES, axis=0, tiled=True)
    own = jnp.dot(
        teacher, weight.astype(jnp.bfloat16), preferred_element_type=jnp.float32
    ).astype(jnp.bfloat16)
    student = lax.all_gather(own, AXES, axis=0, tiled=True)
    mine = lax.dynamic_index_in_dim(mask_sym, here, 0, keepdims=False)
    per_item = jnp.broadcast_to((mine / width)[:, None], (wide, block)).reshape(1, n)
    same = (item_group[:, None] == group[None, :]).astype(jnp.float32)
    stud = lax.dot_general(own, student, NT, preferred_element_type=jnp.float32)
    near = jnp.dot(
        (per_item * (1.0 + same) * stud).astype(jnp.bfloat16),
        student,
        preferred_element_type=jnp.float32,
    )
    far = pair_part(mask_sym * (-1.0 / d), columns, student, group, block)
    far = lax.all_to_all(far.reshape(count, rows, width), AXES, split_axis=0, concat_axis=0, tiled=True)
    total = near + jnp.sum(far.astype(jnp.float32), axis=0)
    grad = (total * (2.0 * d / (n * width))).astype(jnp.bfloat16)
    grad = lax.all_gather(grad, AXES, axis=0, tiled=True)
    return lax.dot_general(columns, grad, TN, preferred_element_type=jnp.float32)


def solution(mesh):
    in_specs = (P(("parts",) + AXES, None), P(), P("parts", None), P(("parts",) + AXES))
    return jax.shard_map(
        per_device,
        mesh=mesh,
        in_specs=in_specs,
        out_specs=P(("parts",) + AXES, None),
        check_vma=False,
    )
```

```python
import functools

import jax
import jax.numpy as jnp
from jax import lax
from jax.experimental import pallas as pl
from jax.experimental.pallas import tpu as pltpu
from jax.sharding import PartitionSpec as P

AXES = ("wide", "narrow")
NT = (((1,), (1,)), ((), ()))
TN = (((0,), (0,)), ((), ()))


def pair_kernel(block, blocks, mask_ref, rows_ref, all_ref, stud_ref, gcol_ref, grow_ref, out_ref):
    tile = rows_ref.shape[0]
    mine = pl.program_id(0) * tile // block
    rows = rows_ref[...]
    gcol = gcol_ref[...]

    def step(b, acc):
        cols = pl.ds(pl.multiple_of(b * block, block), block)
        e = lax.dot_general(rows, all_ref[cols, :], NT, preferred_element_type=jnp.float32)
        f = mask_ref[mine, b]
        w = jnp.where(gcol == grow_ref[:, cols], 2.0 * f, f)
        p = (e * w).astype(jnp.bfloat16)
        return acc + jnp.dot(p, stud_ref[cols, :], preferred_element_type=jnp.float32)

    acc = lax.fori_loop(
        0, blocks, step, jnp.zeros((tile, stud_ref.shape[1]), jnp.float32), unroll=blocks <= 4
    )
    out_ref[...] = acc.astype(jnp.bfloat16)


def pair_part(mask_sym, columns, student, group, block):
    n, dc = columns.shape
    p = student.shape[1]
    tile = block // 2
    blocks = n // block
    whole = lambda i: (0, 0)
    mine = lambda i: (i, 0)
    return pl.pallas_call(
        functools.partial(pair_kernel, block, blocks),
        grid=(n // tile,),
        in_specs=[
            pl.BlockSpec(memory_space=pltpu.SMEM),
            pl.BlockSpec((tile, dc), mine),
            pl.BlockSpec((n, dc), whole),
            pl.BlockSpec((n, p), whole),
            pl.BlockSpec((tile, 1), mine),
            pl.BlockSpec((1, n), whole),
        ],
        out_specs=pl.BlockSpec((tile, p), mine),
        out_shape=jax.ShapeDtypeStruct((n, p), jnp.bfloat16),
        compiler_params=pltpu.CompilerParams(vmem_limit_bytes=48 * 2**20),
        cost_estimate=pl.CostEstimate(
            flops=2 * n * n * (dc + p), bytes_accessed=2 * n * (dc + 2 * p), transcendentals=0
        ),
    )(mask_sym, columns, columns, student, group.reshape(n, 1), group.reshape(1, n))


def ring_kernel(
    wide, teacher_hbm, weight_hbm, mask, group, out,
    teacher, weight, cols, stud, groups, far_out, c_in, x_out, x_in, z_out, z_in, grads, flipped,
    t_send, t_recv, g_send, g_recv, c_send, c_recv, x_send, x_recv, z_send, z_recv,
    s_send, s_recv, d_send, d_recv, local,
):
    rows, d = teacher.shape
    loads = [
        pltpu.make_async_copy(teacher_hbm, teacher, local.at[0]),
        pltpu.make_async_copy(weight_hbm, weight, local.at[1]),
    ]
    for load in loads:
        load.start()
    dc = cols.shape[1]
    count = wide * 4
    w, nn = lax.axis_index("wide"), lax.axis_index("narrow")
    me = w * 4 + nn
    core = nn % 2

    def at(i):
        return pl.ds(pl.multiple_of(i * rows, rows), rows)

    def dev(i):
        return {"wide": i // 4, "narrow": i % 4}

    def remote(source, target, send, recv, i):
        return pltpu.make_async_remote_copy(
            src_ref=source, dst_ref=target, send_sem=send, recv_sem=recv,
            device_id=dev(i), device_id_type=pl.DeviceIdType.MESH,
        )

    barrier = pltpu.get_barrier_semaphore()

    @pl.loop(1, count)
    def _(k):
        pl.semaphore_signal(
            barrier, inc=1, device_id=dev((me + k) % count), device_id_type=pl.DeviceIdType.MESH
        )

    pl.semaphore_wait(barrier, count - 1)

    def column_copy(peer, origin, k):
        part = pl.ds(pl.multiple_of(peer * dc, dc), dc)
        return remote(teacher_hbm.at[:, part], cols.at[at(origin), :], t_send.at[k], t_recv.at[k], peer)

    def group_copy(peer, origin, k):
        return remote(group.at[0], groups.at[origin], g_send.at[k], g_recv.at[k], peer)

    @pl.loop(1, count)
    def _(k):
        group_copy((me + k) % count, me, k).start()

    def send_columns(first, last):
        @pl.loop(first, last)
        def _(i):
            k = 1 + (i + 6) % (count - 1)
            column_copy((me + k) % count, me, k).start()

    send_columns(0, 5)

    for load in loads:
        load.wait()
    cols[at(me), :] = teacher[:, pl.ds(pl.multiple_of(me * dc, dc), dc)]
    groups[me] = group[0]

    step = 512

    def project(c, acc):
        part = pl.ds(pl.multiple_of(c * step, step), step)
        return acc + jnp.dot(
            teacher[:, part],
            weight[part, :].astype(jnp.bfloat16),
            preferred_element_type=jnp.float32,
        )

    own = lax.fori_loop(
        0, d // step, project, jnp.zeros((rows, stud.shape[1]), jnp.float32)
    )
    stud[at(me), :] = own.astype(jnp.bfloat16)

    def gather(buf, send, recv, use, then):
        nx = (nn + 2) % 4
        nc = nn + 1 - 2 * core
        ncx = (nc + 2) % 4

        def copy(origin_w, origin_n, slot, to):
            part = buf.at[at(origin_w * 4 + origin_n), :]
            return remote(part, part, send.at[slot], recv.at[slot], to)

        sent = []

        def go(*args):
            c = copy(*args)
            c.start()
            sent.append(c)

        def landed(*args):
            copy(*args, me).wait_recv()

        a, b, c1, c2 = 0, wide, 2 * wide, 3 * wide
        planes = [w, w + 1 - 2 * (w % 2), (w + 2) % 4, 3 - w]
        for j in (3, 2, 1):
            go(w, nn, a + j, planes[j] * 4 + nn)
        go(w, nn, b, w * 4 + nx)
        go(w, nn, c1, w * 4 + nc)
        then()
        landed(w, nx, b)
        go(w, nx, c2, w * 4 + nc)
        for j in range(1, wide):
            landed(planes[j], nn, a + j)
            go(planes[j], nn, b + j, w * 4 + nx)
            go(planes[j], nn, c1 + j, w * 4 + nc)
            if j == 1:
                landed(w, nc, c1)
                landed(w, ncx, c2)
                use(w)
        for j in range(1, wide):
            landed(planes[j], nx, b + j)
            go(planes[j], nx, c2 + j, w * 4 + nc)
        for j in range(1, wide):
            landed(planes[j], nc, c1 + j)
            landed(planes[j], ncx, c2 + j)
            use(planes[j])
        for c in sent:
            c.wait_send()

    def send_rest():
        send_columns(5, 9)
        send_columns(12, count - 1)
        send_columns(9, 12)

    gather(stud, s_send, s_recv, lambda plane: None, send_rest)

    @pl.loop(1, count)
    def _(k):
        origin = (me + count - k) % count
        column_copy(me, origin, k).wait_recv()
        group_copy(me, origin, k).wait_recv()

    def weights(gcol, b, f):
        return jnp.concatenate(
            [jnp.where(gcol == groups[b * 4 + i].astype(jnp.float32), 2.0 * f, f) for i in range(4)], axis=1
        )

    def spread(i):
        return jnp.broadcast_to(groups[i].astype(jnp.float32), (rows, rows)).T

    def terms(left, all_rows, gcol, mine, scale):
        acc = jnp.zeros((left.shape[0], stud.shape[1]), jnp.float32)
        for b in range(wide):
            span = pl.ds(b * 4 * rows, 4 * rows)
            e = lax.dot_general(left, all_rows[span, :], NT, preferred_element_type=jnp.float32)
            f = (mask[mine, b] + mask[b, mine]).astype(jnp.float32) * scale
            p = (e * weights(gcol, b, f)).astype(jnp.bfloat16)
            acc = acc + jnp.dot(p, stud[span, :], preferred_element_type=jnp.float32)
        return acc

    x = nn // 2
    other = 1 - core
    width = stud.shape[1]
    steps = [(j, 1 - x) for j in (2, 1, 3, 4)] + [(j, x) for j in (2, 1, 3, 4)]

    def slot(i):
        return pl.ds(i * rows, rows)

    def half(i, c):
        return pl.ds(pl.multiple_of((2 * i + c) * rows, rows), rows)

    def core_copy(i):
        return remote(
            far_out.at[half(i, other), :], c_in.at[slot(i), :],
            c_send.at[i], c_recv.at[i], w * 4 + nn + 1 - 2 * core,
        )

    def x_copy(j):
        return remote(
            x_out.at[slot(j - 1), :], x_in.at[slot(j - 1), :],
            x_send.at[j - 1], x_recv.at[j - 1], w * 4 + (nn + 2) % 4,
        )

    def z_copy(j):
        return remote(
            z_out.at[slot(j - 1), :], z_in.at[slot(j - 1), :],
            z_send.at[j - 1], z_recv.at[j - 1], (w + j) % wide * 4 + nn,
        )

    def compute(i):
        j, to_x = steps[i]
        q = (w + j) % wide * 2 + to_x
        pair = pl.ds(pl.multiple_of(q * 2 * rows, 2 * rows), 2 * rows)
        gcol = jnp.concatenate([spread(2 * q), spread(2 * q + 1)], axis=0)
        far_out[pl.ds(2 * i * rows, 2 * rows), :] = terms(
            cols[pair, :], cols, gcol, q // 2, -1.0 / d
        ).astype(jnp.bfloat16)
        core_copy(i).start()

    def finish(i):
        j, _ = steps[i]
        core_copy(i).wait_recv()
        part = far_out[half(i, core), :].astype(jnp.float32)
        part = part + c_in[slot(i), :].astype(jnp.float32)
        if i < wide:
            x_out[slot(j - 1), :] = part.astype(jnp.bfloat16)
            x_copy(j).start()
            return None
        x_copy(j).wait_recv()
        part = part + x_in[slot(j - 1), :].astype(jnp.float32)
        if j < wide:
            z_out[slot(j - 1), :] = part.astype(jnp.bfloat16)
            z_copy(j).start()
        return part

    for i in range(2 * wide):
        compute(i)
        if i:
            finish(i - 1)
    total = terms(stud[at(me), :], stud, spread(me), w, 1.0 / width)
    total = total + finish(2 * wide - 1)
    for b in range(wide):
        span = pl.ds(b * 4 * rows, 4 * rows)
        flipped[:, span] = cols[span, :].T
    for j in range(1, wide):
        z_copy(j).wait_recv()
        total = total + z_in[slot(j - 1), :].astype(jnp.float32)
    grads[at(me), :] = (total * (2.0 * d / (rows * count * width))).astype(jnp.bfloat16)
    out[...] = jnp.zeros_like(out)

    def use(plane):
        span = pl.ds(pl.multiple_of(plane * 4 * rows, 4 * rows), 4 * rows)
        out[...] += jnp.dot(flipped[:, span], grads[span, :], preferred_element_type=jnp.float32)

    gather(grads, d_send, d_recv, use, lambda: None)

    @pl.loop(1, count)
    def _(k):
        peer = (me + k) % count
        column_copy(peer, me, k).wait_send()
        group_copy(peer, me, k).wait_send()

    for i in range(2 * wide):
        core_copy(i).wait_send()
    for j in range(1, wide + 1):
        x_copy(j).wait_send()
    for j in range(1, wide):
        z_copy(j).wait_send()


def in_one(teacher, weight, block_mask, item_group, wide):
    rows, d = teacher.shape
    width = weight.shape[1]
    count = wide * 4
    n = rows * count
    dc = d // count
    vmem = pl.BlockSpec(memory_space=pltpu.VMEM)
    hbm = pl.BlockSpec(memory_space=pltpu.HBM)
    sem = pltpu.SemaphoreType.DMA
    return pl.pallas_call(
        functools.partial(ring_kernel, wide),
        in_specs=[hbm, hbm, pl.BlockSpec(memory_space=pltpu.SMEM), vmem],
        out_specs=vmem,
        out_shape=jax.ShapeDtypeStruct((dc, width), jnp.float32),
        scratch_shapes=[
            pltpu.VMEM((rows, d), jnp.bfloat16),
            pltpu.VMEM((d, width), jnp.float32),
            pltpu.VMEM((n, dc), jnp.bfloat16),
            pltpu.VMEM((n, width), jnp.bfloat16),
            pltpu.VMEM((count, 1, rows), jnp.int32),
            pltpu.VMEM((n, width), jnp.bfloat16),
            pltpu.VMEM((2 * wide * rows, width), jnp.bfloat16),
        ]
        + [pltpu.VMEM((wide * rows, width), jnp.bfloat16)] * 4
        + [pltpu.VMEM((n, width), jnp.bfloat16), pltpu.VMEM((dc, n), jnp.bfloat16)]
        + [sem((count,))] * 4
        + [sem((2 * wide,))] * 2
        + [sem((wide,))] * 4
        + [sem((4 * wide,))] * 4
        + [sem((2,))],
        compiler_params=pltpu.CompilerParams(
            collective_id=0, has_side_effects=True, vmem_limit_bytes=62 * 2**20
        ),
    )(teacher, weight, block_mask, item_group.reshape(1, 1, rows))


def per_device(teacher, weight, block_mask, item_group):
    rows, d = teacher.shape
    width = weight.shape[1]
    wide = lax.axis_size("wide")
    count = wide * lax.axis_size("narrow")
    block = rows * lax.axis_size("narrow")
    n = rows * count
    here = lax.axis_index("wide")
    mask = block_mask.astype(jnp.float32)
    mask_sym = mask + mask.T
    if count == 4 * wide and wide == 4 and d % (count * 128) == 0 and rows == 128 and n <= 2048:
        return in_one(teacher, weight, block_mask, item_group, wide)
    columns = lax.all_to_all(teacher, AXES, split_axis=1, concat_axis=0, tiled=True)
    group = lax.all_gather(item_group, AXES, axis=0, tiled=True)
    own = jnp.dot(
        teacher, weight.astype(jnp.bfloat16), preferred_element_type=jnp.float32
    ).astype(jnp.bfloat16)
    student = lax.all_gather(own, AXES, axis=0, tiled=True)
    mine = lax.dynamic_index_in_dim(mask_sym, here, 0, keepdims=False)
    per_item = jnp.broadcast_to((mine / width)[:, None], (wide, block)).reshape(1, n)
    same = (item_group[:, None] == group[None, :]).astype(jnp.float32)
    stud = lax.dot_general(own, student, NT, preferred_element_type=jnp.float32)
    near = jnp.dot(
        (per_item * (1.0 + same) * stud).astype(jnp.bfloat16),
        student,
        preferred_element_type=jnp.float32,
    )
    far = pair_part(mask_sym * (-1.0 / d), columns, student, group, block)
    far = lax.all_to_all(far.reshape(count, rows, width), AXES, split_axis=0, concat_axis=0, tiled=True)
    total = near + jnp.sum(far.astype(jnp.float32), axis=0)
    grad = (total * (2.0 * d / (n * width))).astype(jnp.bfloat16)
    grad = lax.all_gather(grad, AXES, axis=0, tiled=True)
    return lax.dot_general(columns, grad, TN, preferred_element_type=jnp.float32)


def solution(mesh):
    in_specs = (P(("parts",) + AXES, None), P(), P("parts", None), P(("parts",) + AXES))
    return jax.shard_map(
        per_device,
        mesh=mesh,
        in_specs=in_specs,
        out_specs=P(("parts",) + AXES, None),
        check_vma=False,
    )
```
